32 devices in a mesh: dp: 8 (over y, x, core), tensor: 4 (over z).
Axes of the slice: x: 2, y: 2, z: 4, core: 2. Of those that a mesh axis runs over, the one named last changes fastest.
Arguments:
- send_order: int32 [32, 32], P(('dp', 'tensor')), may hold values from 0 to 31, each once within a row
- master: float32 [32, 32, 2048], P(('dp', 'tensor')), may hold values from -6 to 6
- first_code: bfloat16 [32, 32, 2048], P(('dp', 'tensor')), may hold values from -1 to 1
- first_scale: float32 [32, 32], P(('dp', 'tensor')), may hold values from 0.1 to 2
- second_code: bfloat16 [32, 32, 2048], P(('dp', 'tensor')), may hold values from 0.049804688 to 1
- second_scale: float32 [32, 32], P(('dp', 'tensor')), may hold values from 0.5 to 20
- grads: bfloat16 [8, 4, 8, 32, 2048], P('dp', 'tensor'), may hold values from -6 to 6
Outputs:
- new_master: float32 [32, 32, 2048], P(('dp', 'tensor'))
- new_first_code: bfloat16 [32, 32, 2048], P(('dp', 'tensor'))
- new_first_scale: float32 [32, 32], P(('dp', 'tensor'))
- new_second_code: bfloat16 [32, 32, 2048], P(('dp', 'tensor'))
- new_second_scale: float32 [32, 32], P(('dp', 'tensor'))
- weights: bfloat16 [4, 8, 32, 2048], P('tensor')
The draws below stay inside these ranges and needn't reach their ends.
Inputs may be any that keep to these rules, and one draw needn't show every extreme that they name: `send_order`: each row is an ordering of the slots 0 to 31, each once.
All inputs are finite; a program needn't handle non-finite values. Where the reference program divides by a largest or mean magnitude, that divisor is 1e-20 or more.
Results may differ from the reference program's by a relative error of at most 0.001.
Values may be sent and summed in bfloat16 or wider, within the bound.
A program may use at most 128 MiB of HBM per device.

```python
import math
import jax
import jax.numpy as jnp
from jax import lax

BLOCK = 2048
PER = 1
BPD = 32
STEP = 10
N_DP = 8
N_TENSOR = 4
DEVICES = 32


def raised(values, rng, source, target, blocks, factor):
    def block_of(dim):
        return (jnp.arange(values.shape[dim]) // (values.shape[dim] // blocks)).reshape((-1,) + (1,) * (values.ndim - 1 - dim))

    one_side = jax.random.permutation(rng, blocks)[block_of(target)]
    second = (block_of(target) + blocks // 2) % blocks
    return jnp.where((block_of(source) == one_side) | (block_of(source) == second), factor * values, values)


def block_scale(own_key, dims, pieces, smallest, high):
    def one(position, blocks):
        heights = jax.random.uniform(jax.random.fold_in(jax.random.fold_in(own_key, 6), position), (blocks,), jnp.float32, smallest / len(pieces), high / len(pieces))
        return jnp.repeat(jnp.exp(heights), dims[position] // blocks).reshape((-1,) + (1,) * (len(dims) - position - 1))

    level = one(*pieces[0])
    for cut in pieces[1:]:
        level = level * one(*cut)
    return level


def centred(rng, dims, width, most, shards=(), held_as=jnp.bfloat16):
    values = jax.random.normal(rng, dims, jnp.float32) * width
    if len(shards) > 0:
        values = block_scale(rng, dims, shards, -0.22, 0.18) * values
    return jnp.clip(values, min=-most, max=most).astype(held_as)


def noise_with(own_key, extent, spread, bound, shards, heavy, kind=jnp.bfloat16):
    array = spread * jax.random.normal(own_key, extent, jnp.float32)
    if shards:
        array = array * block_scale(own_key, extent, shards, -0.22, 0.18)
    return jnp.clip(raised(array, jax.random.fold_in(own_key, 3), *heavy), -bound, bound).astype(kind)


def setup_inputs(seed: int = 0) -> dict:
    streams_of = jax.random.split(jax.random.key(seed), 8)
    return {
        "send_order": jax.vmap(lambda own: jax.random.permutation(own, BPD))(jax.random.split(streams_of[0], DEVICES)).reshape((DEVICES, BPD)).astype(jnp.int32),
        "master": centred(streams_of[1], (DEVICES, BPD, BLOCK), 1.0, 6.0, ((0, 32),), jnp.float32),
        "first_code": jnp.clip(jax.random.uniform(streams_of[2], (DEVICES, BPD, BLOCK), jnp.float32, -1.0, 1.0) * block_scale(streams_of[2], (DEVICES, BPD, BLOCK), ((0, 32),), -0.4, 0.0), -1.0, 1.0).astype(jnp.bfloat16),
        "first_scale": jnp.clip(jnp.exp(math.log(2.0) - 2.9957323 * jax.random.uniform(streams_of[3], (DEVICES, BPD), jnp.float32) ** block_scale(streams_of[3], (DEVICES, BPD), ((0, 32),), -0.2, 0.2)), 0.1, 2.0),
        "second_code": jnp.clip(0.049804688 + 0.9501953 * jax.random.uniform(streams_of[4], (DEVICES, BPD, BLOCK), jnp.float32) ** block_scale(streams_of[4], (DEVICES, BPD, BLOCK), ((0, 32),), -0.2, 0.2), 0.049804688, 1.0).astype(jnp.bfloat16),
        "second_scale": jnp.clip(jnp.exp(math.log(20.0) - 3.6888795 * jax.random.uniform(streams_of[5], (DEVICES, BPD), jnp.float32) ** block_scale(streams_of[5], (DEVICES, BPD), ((0, 32),), -0.2, 0.2)), 0.5, 20.0),
        "grads": noise_with(streams_of[6], (N_DP, N_TENSOR, N_DP, BPD, BLOCK), 1.0, 6.0, ((0, 8), (1, 4)), (0, 2, 8, 2.0)),
    }


def relay_array(source, send_order):
    rows = jnp.arange(DEVICES, dtype=jnp.int32)[:, None]
    taken = source[rows, send_order]
    rest = taken.shape[2:]
    taken = taken.reshape((DEVICES, DEVICES, PER) + rest)
    taken = jnp.swapaxes(taken, 0, 1)
    return taken.reshape((DEVICES, BPD) + rest)

def reference(send_order, master, first_code, first_scale, second_code, second_scale, grads):
    master_new = relay_array(master, send_order)
    code_one = relay_array(first_code, send_order)
    scale_one = relay_array(first_scale, send_order)
    code_two = relay_array(second_code, send_order)
    scale_two = relay_array(second_scale, send_order)

    def accumulate(total, piece):
        return (total + piece.astype(jnp.float32), None)
    start = jnp.zeros(grads.shape[1:], jnp.float32)
    summed, unused = lax.scan(accumulate, start, grads)
    grad = jnp.swapaxes(summed, 0, 1).reshape(DEVICES, BPD, BLOCK)
    first = code_one.astype(jnp.float32) * scale_one[:, :, None]
    second = code_two.astype(jnp.float32) * scale_two[:, :, None]
    moment_one = 0.9 * first + 0.1 * grad
    moment_two = 0.95 * second + 0.05 * grad * grad
    corr_one = 1.0 - 0.9 ** STEP
    corr_two = 1.0 - 0.95 ** STEP
    update = moment_one / corr_one / (jnp.sqrt(moment_two / corr_two) + 1e-08) + 0.1 * master_new
    new_master = master_new - 0.01 * update
    new_scale_one = lax.optimization_barrier(jnp.max(jnp.abs(moment_one), axis=2)) + 1e-06
    new_code_one = (moment_one / new_scale_one[:, :, None]).astype(jnp.bfloat16)
    new_scale_two = lax.optimization_barrier(jnp.max(jnp.abs(moment_two), axis=2)) + 1e-06
    new_code_two = (moment_two / new_scale_two[:, :, None]).astype(jnp.bfloat16)
    weights = new_master.astype(jnp.bfloat16).reshape(N_DP, N_TENSOR, BPD, BLOCK)
    weights = jnp.swapaxes(weights, 0, 1)
    return (new_master, new_code_one, new_scale_one, new_code_two, new_scale_two, weights)
```

```python
import functools

import jax
import jax.numpy as jnp
from jax import lax
from jax.experimental import pallas as pl
from jax.experimental.pallas import tpu as pltpu
from jax.sharding import PartitionSpec as P

STEP = 10
LANES = 128
PARTS = 2
MESH = pl.DeviceIdType.MESH


def _kernel(nd, nt, slots, width, order_hbm, m_hbm, c1_hbm, s1_hbm, c2_hbm, s2_hbm, g_hbm,
            nm_out, nc1_out, ns1_out, nc2_out, ns2_out, wg,
            order_v, s1_v, s2_v, m_v, c1_v, c2_v,
            xs_m, xs_f, xs_c, xs_s, xr_m, xr_c, xr_s, gr, m1_v, m2_v,
            in_sem, rm, rc, rs, rg, sm, sc, ss, sg, ra, sa, rf, sf, lg):
    n = nd * nt
    per = slots // n
    chunks = width // LANES
    cp = chunks // PARTS
    wp = width // PARTS
    half_m = slots * cp
    half_c = slots * 2 * cp
    peers = nd // 2 - 1
    my_dp = lax.axis_index("dp")
    my_t = lax.axis_index("tensor")
    me = my_dp * nt + my_t
    partner = my_dp + 1 - 2 * lax.rem(my_dp, 2)

    loads = [
        pltpu.make_async_copy(order_hbm, order_v, in_sem.at[0]),
        pltpu.make_async_copy(s1_hbm, s1_v, in_sem.at[1]),
        pltpu.make_async_copy(s2_hbm, s2_v, in_sem.at[2]),
        pltpu.make_async_copy(m_hbm.at[0], m_v, in_sem.at[3]),
        pltpu.make_async_copy(c1_hbm.at[0], c1_v, in_sem.at[4]),
        pltpu.make_async_copy(c2_hbm.at[0], c2_v, in_sem.at[5]),
    ]
    for item in loads:
        item.start()

    barrier = pltpu.get_barrier_semaphore()

    def greet(k, carry):
        dst = lax.rem(me + k, n)
        pl.semaphore_signal(barrier, inc=1, device_id=(dst // nt, lax.rem(dst, nt)), device_id_type=MESH)
        return carry

    lax.fori_loop(1, n, greet, 0)

    def cols(h):
        return pl.ds(h * wp, wp)

    own_grad = [
        pltpu.make_async_copy(g_hbm.at[0, 0, my_dp, :, cols(h)], gr.at[my_dp, :, cols(h)], rg.at[h])
        for h in range(PARTS)
    ]
    for item in own_grad:
        item.start()

    for item in loads:
        item.wait()
    row = lax.broadcasted_iota(jnp.int32, (slots, slots), 0)
    lane = lax.broadcasted_iota(jnp.int32, (slots, slots), 1)
    eye = row == lane
    order_f = order_v[...].astype(jnp.float32)
    order_col = jnp.sum(jnp.where(eye, order_f, 0.0), axis=1, keepdims=True)
    pick = order_col == lane.astype(jnp.float32)
    s1_col = jnp.sum(jnp.where(pick, s1_v[...], 0.0), axis=1, keepdims=True)
    s2_col = jnp.sum(jnp.where(pick, s2_v[...], 0.0), axis=1, keepdims=True)
    side = lax.broadcasted_iota(jnp.int32, (slots, LANES), 1) < LANES // 2
    xs_s[pl.ds(0, slots, stride=8), :] = jnp.where(side, s1_col, s2_col)
    select = jnp.where(pick, 1.0, 0.0).astype(jnp.bfloat16)

    def take(x):
        return jnp.dot(select, x, preferred_element_type=jnp.float32)

    def stage(h):
        x = m_v[:, cols(h)]
        hi = x.astype(jnp.bfloat16)
        rest = x - hi.astype(jnp.float32)
        mid = rest.astype(jnp.bfloat16)
        low = (rest - mid.astype(jnp.float32)).astype(jnp.bfloat16)
        xm = (take(hi) + take(mid)) + take(low)
        x1 = take(c1_v[:, cols(h)])
        x2 = take(c2_v[:, cols(h)])
        for j in range(cp):
            piece = slice(j * LANES, (j + 1) * LANES)
            xs_m[pl.ds(h * half_m + j, slots, stride=cp), :] = xm[:, piece]
            xs_f[pl.ds(h * half_c + j, slots, stride=2 * cp), :] = x1[:, piece]
            xs_f[pl.ds(h * half_c + cp + j, slots, stride=2 * cp), :] = x2[:, piece]
        xs_c[pl.ds(h * half_c, half_c), :] = xs_f[pl.ds(h * half_c, half_c), :].astype(jnp.bfloat16)

    stage(0)

    pl.semaphore_wait(barrier, n - 1)

    def send_grads(h):
        def one(k, carry):
            dst = lax.rem(my_dp + k, nd)
            pltpu.make_async_remote_copy(
                src_ref=g_hbm.at[0, 0, dst, :, cols(h)], dst_ref=gr.at[my_dp, :, cols(h)],
                send_sem=sg.at[h], recv_sem=rg.at[h], device_id=(dst, my_t), device_id_type=MESH,
            ).start()
            return carry

        lax.fori_loop(1, nd, one, 0)

    bm = per * cp
    bc = per * 2 * cp
    bs = per * 8

    def send_blocks(h):
        def one(k, carry):
            dst = lax.rem(me + k, n)
            where = (dst // nt, lax.rem(dst, nt))
            pltpu.make_async_remote_copy(
                src_ref=xs_m.at[pl.ds(pl.multiple_of(h * half_m + dst * bm, 8), bm)],
                dst_ref=xr_m.at[pl.ds(pl.multiple_of(h * half_m + me * bm, 8), bm)],
                send_sem=sm.at[h], recv_sem=rm.at[h], device_id=where, device_id_type=MESH,
            ).start()
            pltpu.make_async_remote_copy(
                src_ref=xs_c.at[pl.ds(pl.multiple_of(h * half_c + dst * bc, 16), bc)],
                dst_ref=xr_c.at[pl.ds(pl.multiple_of(h * half_c + me * bc, 16), bc)],
                send_sem=sc.at[h], recv_sem=rc.at[h], device_id=where, device_id_type=MESH,
            ).start()
            if h == 0:
                pltpu.make_async_remote_copy(
                    src_ref=xs_s.at[pl.ds(pl.multiple_of(dst * bs, 8), bs)],
                    dst_ref=xr_s.at[pl.ds(pl.multiple_of(me * bs, 8), bs)],
                    send_sem=ss.at[0], recv_sem=rs.at[0], device_id=where, device_id_type=MESH,
                ).start()
            return carry

        lax.fori_loop(1, n, one, 0)
        at_m = pl.ds(pl.multiple_of(h * half_m + me * bm, 8), bm)
        at_c = pl.ds(pl.multiple_of(h * half_c + me * bc, 16), bc)
        pltpu.make_async_copy(xs_m.at[at_m], xr_m.at[at_m], rm.at[h]).start()
        pltpu.make_async_copy(xs_c.at[at_c], xr_c.at[at_c], rc.at[h]).start()
        if h == 0:
            at_s = pl.ds(pl.multiple_of(me * bs, 8), bs)
            pltpu.make_async_copy(xs_s.at[at_s], xr_s.at[at_s], rs.at[0]).start()

    def drain(ref, sem):
        pltpu.make_async_copy(ref, ref, sem).wait()

    send_grads(0)
    send_blocks(0)
    for h in range(1, PARTS):
        stage(h)
        send_blocks(h)
        send_grads(h)

    inv_one = 1.0 / (1.0 - 0.9**STEP)
    inv_two = 1.0 / (1.0 - 0.95**STEP)

    def adam(h, s1, s2, tops):
        drain(xr_m.at[pl.ds(h * half_m, half_m)], rm.at[h])
        drain(xr_c.at[pl.ds(h * half_c, half_c)], rc.at[h])
        drain(gr.at[:, :, cols(h)], rg.at[h])
        xs_f[pl.ds(h * half_c, half_c), :] = xr_c[pl.ds(h * half_c, half_c), :].astype(jnp.float32)
        top1, top2 = tops
        for j in range(cp):
            at = slice((h * cp + j) * LANES, (h * cp + j + 1) * LANES)
            grad = gr[0, :, at].astype(jnp.float32)
            for p in range(1, nd):
                grad = grad + gr[p, :, at].astype(jnp.float32)
            first = xs_f[pl.ds(h * half_c + j, slots, stride=2 * cp), :] * s1
            second = xs_f[pl.ds(h * half_c + cp + j, slots, stride=2 * cp), :] * s2
            old = xr_m[pl.ds(h * half_m + j, slots, stride=cp), :]
            one = 0.9 * first + 0.1 * grad
            two = 0.95 * second + 0.05 * grad * grad
            update = (one * inv_one) / (jnp.sqrt(two * inv_two) + 1e-08) + 0.1 * old
            new = old - 0.01 * update
            nm_out[0, :, at] = new
            wg[0, my_dp, :, at] = new.astype(jnp.bfloat16)
            m1_v[:, at] = one
            m2_v[:, at] = two
            top1 = jnp.maximum(top1, jnp.abs(one))
            top2 = jnp.maximum(top2, jnp.abs(two))
        return top1, top2

    def gathered(src, h):
        return wg.at[0, src, :, cols(h)]

    def to_peer(h, j):
        dst = lax.rem(my_dp + 2 * j, nd)
        return pltpu.make_async_remote_copy(
            src_ref=gathered(my_dp, h), dst_ref=gathered(my_dp, h),
            send_sem=sa.at[h, j], recv_sem=ra.at[h, j], device_id=(dst, my_t), device_id_type=MESH,
        )

    def to_partner(h, j):
        src = lax.rem(my_dp + nd - 2 * j, nd)
        return pltpu.make_async_remote_copy(
            src_ref=gathered(src, h), dst_ref=gathered(src, h),
            send_sem=sf.at[h, j], recv_sem=rf.at[h, j], device_id=(partner, my_t), device_id_type=MESH,
        )

    def forward(h):
        for j in range(1, peers + 1):
            to_peer(h, j).wait_recv()
            to_partner(h, j).start()

    drain(xr_s, rs.at[0])
    got = xr_s[pl.ds(0, slots, stride=8), :]
    s1 = got[:, 0:1]
    s2 = got[:, LANES // 2:LANES // 2 + 1]
    zero = jnp.zeros((slots, LANES), jnp.float32)
    tops = (zero, zero)
    for h in range(PARTS):
        tops = adam(h, s1, s2, tops)
        for j in range(1, peers + 1):
            to_peer(h, j).start()
        to_partner(h, 0).start()
        if h > 0:
            forward(h - 1)

    top1 = jnp.max(tops[0], axis=1, keepdims=True) + 1e-06
    top2 = jnp.max(tops[1], axis=1, keepdims=True) + 1e-06
    ns1_out[...] = jnp.sum(jnp.where(eye, top1, 0.0), axis=0, keepdims=True)
    ns2_out[...] = jnp.sum(jnp.where(eye, top2, 0.0), axis=0, keepdims=True)
    inv1 = 1.0 / top1
    inv2 = 1.0 / top2
    for j in range(chunks):
        at = slice(j * LANES, (j + 1) * LANES)
        nc1_out[0, :, at] = (m1_v[:, at] * inv1).astype(jnp.bfloat16)
        nc2_out[0, :, at] = (m2_v[:, at] * inv2).astype(jnp.bfloat16)

    forward(PARTS - 1)
    for h in range(PARTS):
        for j in range(peers + 1):
            to_partner(h, j).wait()
        for j in range(1, peers + 1):
            to_peer(h, j).wait_send()
        drain(xs_m.at[pl.ds(0, half_m - bm)], sm.at[h])
        drain(xs_c.at[pl.ds(0, half_c - bc)], sc.at[h])
        drain(gr.at[pl.ds(0, nd - 1), :, cols(h)], sg.at[h])
    drain(xs_s.at[pl.ds(0, slots * 8 - bs)], ss.at[0])


def on_device(send_order, master, first_code, first_scale, second_code, second_scale, grads):
    nd = lax.axis_size("dp")
    nt = lax.axis_size("tensor")
    slots = master.shape[1]
    width = master.shape[2]
    f32, b16 = jnp.float32, jnp.bfloat16
    rows = slots * width // LANES
    dma = pltpu.SemaphoreType.DMA
    ring = nd // 2
    return pl.pallas_call(
        functools.partial(_kernel, nd, nt, slots, width),
        out_shape=(
            jax.ShapeDtypeStruct((1, slots, width), f32),
            jax.ShapeDtypeStruct((1, slots, width), b16),
            jax.ShapeDtypeStruct((1, slots), f32),
            jax.ShapeDtypeStruct((1, slots, width), b16),
            jax.ShapeDtypeStruct((1, slots), f32),
            jax.ShapeDtypeStruct((1, nd, slots, width), b16),
        ),
        in_specs=[pl.BlockSpec(memory_space=pl.ANY)] * 7,
        out_specs=[pl.BlockSpec(memory_space=pltpu.VMEM)] * 6,
        scratch_shapes=[
            pltpu.VMEM((1, slots), jnp.int32),
            pltpu.VMEM((1, slots), f32),
            pltpu.VMEM((1, slots), f32),
            pltpu.VMEM((slots, width), f32),
            pltpu.VMEM((slots, width), b16),
            pltpu.VMEM((slots, width), b16),
            pltpu.VMEM((rows, LANES), f32),
            pltpu.VMEM((2 * rows, LANES), f32),
            pltpu.VMEM((2 * rows, LANES), b16),
            pltpu.VMEM((slots * 8, LANES), f32),
            pltpu.VMEM((rows, LANES), f32),
            pltpu.VMEM((2 * rows, LANES), b16),
            pltpu.VMEM((slots * 8, LANES), f32),
            pltpu.VMEM((nd, slots, width), b16),
            pltpu.VMEM((slots, width), f32),
            pltpu.VMEM((slots, width), f32),
            dma((6,)),
            dma((PARTS,)), dma((PARTS,)), dma((1,)), dma((PARTS,)),
            dma((PARTS,)), dma((PARTS,)), dma((1,)), dma((PARTS,)),
            dma((PARTS, ring)), dma((PARTS, ring)), dma((PARTS, ring)), dma((PARTS, ring)),
            dma((1,)),
        ],
        compiler_params=pltpu.CompilerParams(collective_id=0, has_side_effects=True),
        name="relayout_adam",
    )(send_order, master, first_code, first_scale, second_code, second_scale, grads)


def solution(mesh):
    placed = (
        P(("dp", "tensor"), None),
        P(("dp", "tensor"), None, None),
        P(("dp", "tensor"), None, None),
        P(("dp", "tensor"), None),
        P(("dp", "tensor"), None, None),
        P(("dp", "tensor"), None),
        P("dp", "tensor", None, None, None),
    )
    return jax.shard_map(
        on_device,
        mesh=mesh,
        in_specs=placed,
        out_specs=(
            P(("dp", "tensor"), None, None),
            P(("dp", "tensor"), None, None),
            P(("dp", "tensor"), None),
            P(("dp", "tensor"), None, None),
            P(("dp", "tensor"), None),
            P("tensor", None, None, None),
        ),
        check_vma=False,
    )
```

```python
import functools

import jax
import jax.numpy as jnp
from jax import lax
from jax.experimental import pallas as pl
from jax.experimental.pallas import tpu as pltpu
from jax.sharding import PartitionSpec as P

STEP = 10
LANES = 128
PARTS = 2
MESH = pl.DeviceIdType.MESH


def _kernel(nd, nt, slots, width, order_hbm, m_hbm, c1_hbm, s1_hbm, c2_hbm, s2_hbm, g_hbm,
            nm_out, nc1_out, ns1_out, nc2_out, ns2_out, wg,
            order_v, s1_v, s2_v, m_v, c1_v, c2_v,
            xs_m, xs_f, xs_c, xs_s, xr_m, xr_c, xr_s, gr, m1_v, m2_v,
            in_sem, rm, rc, rs, rg, sm, sc, ss, sg, ra, sa, rf, sf):
    n = nd * nt
    per = slots // n
    chunks = width // LANES
    cp = chunks // PARTS
    wp = width // PARTS
    half_m = slots * cp
    half_c = slots * 2 * cp
    peers = nd // 2 - 1
    my_dp = lax.axis_index("dp")
    my_t = lax.axis_index("tensor")
    me = my_dp * nt + my_t
    partner = my_dp + 1 - 2 * lax.rem(my_dp, 2)

    loads = [
        pltpu.make_async_copy(order_hbm, order_v, in_sem.at[0]),
        pltpu.make_async_copy(s1_hbm, s1_v, in_sem.at[1]),
        pltpu.make_async_copy(s2_hbm, s2_v, in_sem.at[2]),
        pltpu.make_async_copy(m_hbm.at[0], m_v, in_sem.at[3]),
        pltpu.make_async_copy(c1_hbm.at[0], c1_v, in_sem.at[4]),
        pltpu.make_async_copy(c2_hbm.at[0], c2_v, in_sem.at[5]),
    ]
    for item in loads:
        item.start()

    barrier = pltpu.get_barrier_semaphore()

    def greet(k, carry):
        dst = lax.rem(me + k, n)
        pl.semaphore_signal(barrier, inc=1, device_id=(dst // nt, lax.rem(dst, nt)), device_id_type=MESH)
        return carry

    lax.fori_loop(1, n, greet, 0)

    def cols(h):
        return pl.ds(h * wp, wp)

    own_grad = [
        pltpu.make_async_copy(g_hbm.at[0, 0, my_dp, :, cols(h)], gr.at[my_dp, :, cols(h)], rg.at[h])
        for h in range(PARTS)
    ]
    for item in own_grad:
        item.start()

    for item in loads:
        item.wait()
    row = lax.broadcasted_iota(jnp.int32, (slots, slots), 0)
    lane = lax.broadcasted_iota(jnp.int32, (slots, slots), 1)
    eye = row == lane
    order_f = order_v[...].astype(jnp.float32)
    order_col = jnp.sum(jnp.where(eye, order_f, 0.0), axis=1, keepdims=True)
    pick = order_col == lane.astype(jnp.float32)
    s1_col = jnp.sum(jnp.where(pick, s1_v[...], 0.0), axis=1, keepdims=True)
    s2_col = jnp.sum(jnp.where(pick, s2_v[...], 0.0), axis=1, keepdims=True)
    side = lax.broadcasted_iota(jnp.int32, (slots, LANES), 1) < LANES // 2
    xs_s[:, 0, :] = jnp.where(side, s1_col, s2_col)
    select = jnp.where(pick, 1.0, 0.0).astype(jnp.bfloat16)

    def take(x):
        return jnp.dot(select, x, preferred_element_type=jnp.float32)

    def stage(h):
        x = m_v[:, cols(h)]
        hi = x.astype(jnp.bfloat16)
        rest = x - hi.astype(jnp.float32)
        mid = rest.astype(jnp.bfloat16)
        low = (rest - mid.astype(jnp.float32)).astype(jnp.bfloat16)
        xm = (take(hi) + take(mid)) + take(low)
        x1 = take(c1_v[:, cols(h)])
        x2 = take(c2_v[:, cols(h)])
        for j in range(cp):
            piece = slice(j * LANES, (j + 1) * LANES)
            xs_m[pl.ds(h * half_m + j, slots, stride=cp), :] = xm[:, piece]
            xs_f[pl.ds(h * half_c + j, slots, stride=2 * cp), :] = x1[:, piece]
            xs_f[pl.ds(h * half_c + cp + j, slots, stride=2 * cp), :] = x2[:, piece]
        xs_c[pl.ds(h * half_c, half_c), :] = xs_f[pl.ds(h * half_c, half_c), :].astype(jnp.bfloat16)

    stage(0)

    pl.semaphore_wait(barrier, n - 1)

    def send_grads(h):
        def one(k, carry):
            dst = lax.rem(my_dp + k, nd)
            pltpu.make_async_remote_copy(
                src_ref=g_hbm.at[0, 0, dst, :, cols(h)], dst_ref=gr.at[my_dp, :, cols(h)],
                send_sem=sg.at[h], recv_sem=rg.at[h], device_id=(dst, my_t), device_id_type=MESH,
            ).start()
            return carry

        lax.fori_loop(1, nd, one, 0)

    bm = per * cp
    bc = per * 2 * cp
    bs = per

    def send_blocks(h):
        def one(k, carry):
            dst = lax.rem(me + k, n)
            where = (dst // nt, lax.rem(dst, nt))
            pltpu.make_async_remote_copy(
                src_ref=xs_m.at[pl.ds(pl.multiple_of(h * half_m + dst * bm, 8), bm)],
                dst_ref=xr_m.at[pl.ds(pl.multiple_of(h * half_m + me * bm, 8), bm)],
                send_sem=sm.at[h], recv_sem=rm.at[h], device_id=where, device_id_type=MESH,
            ).start()
            pltpu.make_async_remote_copy(
                src_ref=xs_c.at[pl.ds(pl.multiple_of(h * half_c + dst * bc, 16), bc)],
                dst_ref=xr_c.at[pl.ds(pl.multiple_of(h * half_c + me * bc, 16), bc)],
                send_sem=sc.at[h], recv_sem=rc.at[h], device_id=where, device_id_type=MESH,
            ).start()
            if h == 0:
                pltpu.make_async_remote_copy(
                    src_ref=xs_s.at[pl.ds(dst * bs, bs)],
                    dst_ref=xr_s.at[pl.ds(me * bs, bs)],
                    send_sem=ss.at[0], recv_sem=rs.at[0], device_id=where, device_id_type=MESH,
                ).start()
            return carry

        lax.fori_loop(1, n, one, 0)
        at_m = pl.ds(pl.multiple_of(h * half_m + me * bm, 8), bm)
        at_c = pl.ds(pl.multiple_of(h * half_c + me * bc, 16), bc)
        pltpu.make_async_copy(xs_m.at[at_m], xr_m.at[at_m], rm.at[h]).start()
        pltpu.make_async_copy(xs_c.at[at_c], xr_c.at[at_c], rc.at[h]).start()
        if h == 0:
            at_s = pl.ds(me * bs, bs)
            pltpu.make_async_copy(xs_s.at[at_s], xr_s.at[at_s], rs.at[0]).start()

    def drain(ref, sem):
        pltpu.make_async_copy(ref, ref, sem).wait()

    send_grads(0)
    send_blocks(0)
    for h in range(1, PARTS):
        stage(h)
        send_blocks(h)
        send_grads(h)

    inv_one = 1.0 / (1.0 - 0.9**STEP)
    inv_two = 1.0 / (1.0 - 0.95**STEP)

    def adam(h, s1, s2, tops):
        drain(xr_m.at[pl.ds(h * half_m, half_m)], rm.at[h])
        drain(xr_c.at[pl.ds(h * half_c, half_c)], rc.at[h])
        drain(gr.at[:, :, cols(h)], rg.at[h])
        xs_f[pl.ds(h * half_c, half_c), :] = xr_c[pl.ds(h * half_c, half_c), :].astype(jnp.float32)
        top1, top2 = tops
        for j in range(cp):
            at = slice((h * cp + j) * LANES, (h * cp + j + 1) * LANES)
            grad = gr[0, :, at].astype(jnp.float32)
            for p in range(1, nd):
                grad = grad + gr[p, :, at].astype(jnp.float32)
            first = xs_f[pl.ds(h * half_c + j, slots, stride=2 * cp), :] * s1
            second = xs_f[pl.ds(h * half_c + cp + j, slots, stride=2 * cp), :] * s2
            old = xr_m[pl.ds(h * half_m + j, slots, stride=cp), :]
            one = 0.9 * first + 0.1 * grad
            two = 0.95 * second + 0.05 * grad * grad
            update = (one * inv_one) / (jnp.sqrt(two * inv_two) + 1e-08) + 0.1 * old
            new = old - 0.01 * update
            nm_out[0, :, at] = new
            wg[0, my_dp, :, at] = new.astype(jnp.bfloat16)
            m1_v[:, at] = one
            m2_v[:, at] = two
            top1 = jnp.maximum(top1, jnp.abs(one))
            top2 = jnp.maximum(top2, jnp.abs(two))
        return top1, top2

    def gathered(src, h):
        return wg.at[0, src, :, cols(h)]

    def to_peer(h, j):
        dst = lax.rem(my_dp + 2 * j, nd)
        return pltpu.make_async_remote_copy(
            src_ref=gathered(my_dp, h), dst_ref=gathered(my_dp, h),
            send_sem=sa.at[h, j], recv_sem=ra.at[h, j], device_id=(dst, my_t), device_id_type=MESH,
        )

    def to_partner(h, j):
        src = lax.rem(my_dp + nd - 2 * j, nd)
        return pltpu.make_async_remote_copy(
            src_ref=gathered(src, h), dst_ref=gathered(src, h),
            send_sem=sf.at[h, j], recv_sem=rf.at[h, j], device_id=(partner, my_t), device_id_type=MESH,
        )

    def forward(h):
        for j in range(1, peers + 1):
            to_peer(h, j).wait_recv()
            to_partner(h, j).start()

    drain(xr_s, rs.at[0])
    got = xr_s[:, 0, :]
    s1 = got[:, 0:1]
    s2 = got[:, LANES // 2:LANES // 2 + 1]
    zero = jnp.zeros((slots, LANES), jnp.float32)
    tops = (zero, zero)
    for h in range(PARTS):
        tops = adam(h, s1, s2, tops)
        for j in range(1, peers + 1):
            to_peer(h, j).start()
        to_partner(h, 0).start()
        if h > 0:
            forward(h - 1)

    top1 = jnp.max(tops[0], axis=1, keepdims=True) + 1e-06
    top2 = jnp.max(tops[1], axis=1, keepdims=True) + 1e-06
    ns1_out[...] = jnp.sum(jnp.where(eye, top1, 0.0), axis=0, keepdims=True)
    ns2_out[...] = jnp.sum(jnp.where(eye, top2, 0.0), axis=0, keepdims=True)
    inv1 = 1.0 / top1
    inv2 = 1.0 / top2
    for j in range(chunks):
        at = slice(j * LANES, (j + 1) * LANES)
        nc1_out[0, :, at] = (m1_v[:, at] * inv1).astype(jnp.bfloat16)
        nc2_out[0, :, at] = (m2_v[:, at] * inv2).astype(jnp.bfloat16)

    forward(PARTS - 1)
    for h in range(PARTS):
        for j in range(peers + 1):
            to_partner(h, j).wait()
        for j in range(1, peers + 1):
            to_peer(h, j).wait_send()
        drain(xs_m.at[pl.ds(0, half_m - bm)], sm.at[h])
        drain(xs_c.at[pl.ds(0, half_c - bc)], sc.at[h])
        drain(gr.at[pl.ds(0, nd - 1), :, cols(h)], sg.at[h])
    drain(xs_s.at[pl.ds(0, slots - bs)], ss.at[0])


def _write_out(*refs):
    sem = refs[-1]
    count = (len(refs) - 1) // 2
    copies = [pltpu.make_async_copy(refs[i], refs[count + i], sem.at[i]) for i in range(count)]
    for item in copies:
        item.start()
    for item in copies:
        item.wait()


def on_device(send_order, master, first_code, first_scale, second_code, second_scale, grads):
    arrays = (send_order, master, first_code, first_scale, second_code, second_scale, grads)
    nd = lax.axis_size("dp")
    nt = lax.axis_size("tensor")
    slots = master.shape[1]
    width = master.shape[2]
    f32, b16 = jnp.float32, jnp.bfloat16
    rows = slots * width // LANES
    dma = pltpu.SemaphoreType.DMA
    ring = nd // 2
    grant = slots * width * (40 + 2 * nd) + slots * 4096 + 6 * 1024 * 1024
    results = (
        ((1, slots, width), f32),
        ((1, slots, width), b16),
        ((1, slots), f32),
        ((1, slots, width), b16),
        ((1, slots), f32),
        ((1, nd, slots, width), b16),
    )
    held = pl.pallas_call(
        functools.partial(_kernel, nd, nt, slots, width),
        out_shape=tuple(pltpu.VMEM(*item) for item in results),
        in_specs=[pl.BlockSpec(memory_space=pltpu.HBM)] * 7,
        out_specs=[pl.BlockSpec(memory_space=pltpu.VMEM)] * 6,
        scratch_shapes=[
            pltpu.VMEM((1, slots), jnp.int32),
            pltpu.VMEM((1, slots), f32),
            pltpu.VMEM((1, slots), f32),
            pltpu.VMEM((slots, width), f32),
            pltpu.VMEM((slots, width), b16),
            pltpu.VMEM((slots, width), b16),
            pltpu.VMEM((rows, LANES), f32),
            pltpu.VMEM((2 * rows, LANES), f32),
            pltpu.VMEM((2 * rows, LANES), b16),
            pltpu.VMEM((slots, 1, LANES), f32),
            pltpu.VMEM((rows, LANES), f32),
            pltpu.VMEM((2 * rows, LANES), b16),
            pltpu.VMEM((slots, 1, LANES), f32),
            pltpu.VMEM((nd, slots, width), b16),
            pltpu.VMEM((slots, width), f32),
            pltpu.VMEM((slots, width), f32),
            dma((6,)),
            dma((PARTS,)), dma((PARTS,)), dma((1,)), dma((PARTS,)),
            dma((PARTS,)), dma((PARTS,)), dma((1,)), dma((PARTS,)),
            dma((PARTS, ring)), dma((PARTS, ring)), dma((PARTS, ring)), dma((PARTS, ring)),
        ],
        compiler_params=pltpu.CompilerParams(collective_id=0, has_side_effects=True, vmem_limit_bytes=grant),
        name="relayout_adam",
    )(*(pltpu.with_memory_space_constraint(item, pltpu.HBM) for item in arrays))
    return pl.pallas_call(
        _write_out,
        out_shape=tuple(jax.ShapeDtypeStruct(*item) for item in results),
        in_specs=[pl.BlockSpec(memory_space=pltpu.VMEM)] * len(results),
        out_specs=[pl.BlockSpec(memory_space=pltpu.HBM)] * len(results),
        scratch_shapes=[dma((len(results),))],
        compiler_params=pltpu.CompilerParams(vmem_limit_bytes=2 * 1024 * 1024),
        name="write_out",
    )(*(pltpu.with_memory_space_constraint(item, pltpu.VMEM) for item in held))


def solution(mesh):
    placed = (
        P(("dp", "tensor"), None),
        P(("dp", "tensor"), None, None),
        P(("dp", "tensor"), None, None),
        P(("dp", "tensor"), None),
        P(("dp", "tensor"), None, None),
        P(("dp", "tensor"), None),
        P("dp", "tensor", None, None, None),
    )
    return jax.shard_map(
        on_device,
        mesh=mesh,
        in_specs=placed,
        out_specs=(
            P(("dp", "tensor"), None, None),
            P(("dp", "tensor"), None, None),
            P(("dp", "tensor"), None),
            P(("dp", "tensor"), None, None),
            P(("dp", "tensor"), None),
            P("tensor", None, None, None),
        ),
        check_vma=False,
    )
```

```python
import functools

import jax
import jax.numpy as jnp
from jax import lax
from jax.experimental import pallas as pl
from jax.experimental.pallas import tpu as pltpu
from jax.sharding import PartitionSpec as P

STEP = 10
LANES = 128
RELAYS = 2
PARTS = 4
MESH = pl.DeviceIdType.MESH


def _kernel(nd, nt, slots, width, order_hbm, m_hbm, c1_hbm, s1_hbm, c2_hbm, s2_hbm, g_hbm,
            nm_out, nc1_out, ns1_out, nc2_out, ns2_out, wg,
            order_v, s1_v, s2_v, m_v, c1_v, c2_v,
            xs_m, xs_f, xs_c, xs_s, xr_m, xr_c, xr_s, raw_x, raw_y, out_x, out_y, got_x, got_y, m1_v, m2_v,
            in_sem, rm, rc, rs, rg, sm, sc, ss, sg, rh, sh, ra, sa, rf, sf):
    n = nd * nt
    per = slots // n
    chunks = width // LANES
    cp = chunks // RELAYS
    cq = chunks // PARTS
    wr = width // RELAYS
    wp = width // PARTS
    half_m = slots * cp
    half_c = slots * 2 * cp
    ny = nd // 4
    chips = 2 * ny
    my_dp = lax.axis_index("dp")
    my_t = lax.axis_index("tensor")
    me = my_dp * nt + my_t
    my_c = lax.rem(my_dp, 2)
    my_chip = my_dp // 2
    my_x = lax.rem(my_chip, 2)
    my_y = my_chip // 2
    partner = my_dp + 1 - 2 * my_c

    def dp_of(y, x, c):
        return (y * 2 + x) * 2 + c


    loads = [
        pltpu.make_async_copy(order_hbm, order_v, in_sem.at[0]),
        pltpu.make_async_copy(s1_hbm, s1_v, in_sem.at[1]),
        pltpu.make_async_copy(s2_hbm, s2_v, in_sem.at[2]),
        pltpu.make_async_copy(m_hbm.at[0], m_v, in_sem.at[3]),
        pltpu.make_async_copy(c1_hbm.at[0], c1_v, in_sem.at[4]),
        pltpu.make_async_copy(c2_hbm.at[0], c2_v, in_sem.at[5]),
    ]
    for item in loads:
        item.start()

    barrier = pltpu.get_barrier_semaphore()

    def greet(k, carry):
        dst = lax.rem(me + k, n)
        pl.semaphore_signal(barrier, inc=1, device_id=(dst // nt, lax.rem(dst, nt)), device_id_type=MESH)
        return carry

    lax.fori_loop(1, n, greet, 0)

    def cols(h):
        return pl.ds(h * wp, wp)

    def wide(r):
        return pl.ds(r * wr, wr)

    def slabs(h, y, x, c):
        if h % 2 == 0:
            return g_hbm.at[:, x, c, :, cols(h)]
        return g_hbm.at[y, :, c, :, cols(h)]

    def raw_at(h, y, x, c):
        return raw_x.at[h // 2, x, c] if h % 2 == 0 else raw_y.at[h // 2, y, c]

    for h in range(PARTS):
        pltpu.make_async_copy(slabs(h, my_y, my_x, my_c), raw_at(h, my_y, my_x, my_c), rg.at[h]).start()

    for item in loads:
        item.wait()
    row = lax.broadcasted_iota(jnp.int32, (slots, slots), 0)
    lane = lax.broadcasted_iota(jnp.int32, (slots, slots), 1)
    eye = row == lane
    order_f = order_v[...].astype(jnp.float32)
    order_col = jnp.sum(jnp.where(eye, order_f, 0.0), axis=1, keepdims=True)
    pick = order_col == lane.astype(jnp.float32)
    s1_col = jnp.sum(jnp.where(pick, s1_v[...], 0.0), axis=1, keepdims=True)
    s2_col = jnp.sum(jnp.where(pick, s2_v[...], 0.0), axis=1, keepdims=True)
    side = lax.broadcasted_iota(jnp.int32, (slots, LANES), 1) < LANES // 2
    xs_s[:, 0, :] = jnp.where(side, s1_col, s2_col)
    select = jnp.where(pick, 1.0, 0.0).astype(jnp.bfloat16)

    def take(x):
        return jnp.dot(select, x, preferred_element_type=jnp.float32)

    def stage(h):
        x = m_v[:, wide(h)]
        hi = x.astype(jnp.bfloat16)
        rest = x - hi.astype(jnp.float32)
        mid = rest.astype(jnp.bfloat16)
        low = (rest - mid.astype(jnp.float32)).astype(jnp.bfloat16)
        xm = (take(hi) + take(mid)) + take(low)
        x1 = take(c1_v[:, wide(h)])
        x2 = take(c2_v[:, wide(h)])
        for j in range(cp):
            piece = slice(j * LANES, (j + 1) * LANES)
            xs_m[pl.ds(h * half_m + j, slots, stride=cp), :] = xm[:, piece]
            xs_f[pl.ds(h * half_c + j, slots, stride=2 * cp), :] = x1[:, piece]
            xs_f[pl.ds(h * half_c + cp + j, slots, stride=2 * cp), :] = x2[:, piece]
        xs_c[pl.ds(h * half_c, half_c), :] = xs_f[pl.ds(h * half_c, half_c), :].astype(jnp.bfloat16)

    stage(0)

    pl.semaphore_wait(barrier, n - 1)

    def drain(ref, sem):
        pltpu.make_async_copy(ref, ref, sem).wait()

    def send_grads(h):
        group = 2 if h % 2 == 0 else ny

        def one(k, carry):
            step = lax.rem(k, 2 * group)
            c = lax.rem(my_c + step, 2)
            away = step // 2
            if h % 2 == 0:
                y, x = my_y, lax.rem(my_x + away, 2)
            else:
                y, x = lax.rem(my_y + away, ny), my_x
            pltpu.make_async_remote_copy(
                src_ref=slabs(h, y, x, c), dst_ref=raw_at(h, my_y, my_x, my_c),
                send_sem=sg.at[h], recv_sem=rg.at[h], device_id=(dp_of(y, x, c), my_t), device_id_type=MESH,
            ).start()
            return carry

        lax.fori_loop(2, 2 * group, one, 0)
        one(1, 0)

    def second(h):
        return (out_x, got_x, ny, my_y) if h % 2 == 0 else (out_y, got_y, 2, my_x)

    def hand_on(h):
        k = h // 2
        raw = (raw_x if h % 2 == 0 else raw_y).at[k]
        drain(raw, rg.at[h])
        out, got, size, mine = second(h)
        for t in range(size):
            for i in range(cq):
                at = slice(i * LANES, (i + 1) * LANES)
                terms = [raw[u, c, t, :, at].astype(jnp.float32) for u in range(raw.shape[0]) for c in range(2)]
                out[k, t, :, at] = functools.reduce(jnp.add, terms)

        def one(away, carry):
            t = lax.rem(mine + away, size)
            where = dp_of(t, my_x, my_c) if h % 2 == 0 else dp_of(my_y, t, my_c)
            pltpu.make_async_remote_copy(
                src_ref=out.at[k, t], dst_ref=got.at[k, mine],
                send_sem=sh.at[h], recv_sem=rh.at[h], device_id=(where, my_t), device_id_type=MESH,
            ).start()
            return carry

        lax.fori_loop(1, size, one, 0)

    bm = per * cp
    bc = per * 2 * cp
    bs = per

    def send_blocks(h):
        def one(k, carry):
            dst = lax.rem(me + k, n)
            where = (dst // nt, lax.rem(dst, nt))
            pltpu.make_async_remote_copy(
                src_ref=xs_m.at[pl.ds(pl.multiple_of(h * half_m + dst * bm, 8), bm)],
                dst_ref=xr_m.at[pl.ds(pl.multiple_of(h * half_m + me * bm, 8), bm)],
                send_sem=sm.at[h], recv_sem=rm.at[h], device_id=where, device_id_type=MESH,
            ).start()
            pltpu.make_async_remote_copy(
                src_ref=xs_c.at[pl.ds(pl.multiple_of(h * half_c + dst * bc, 16), bc)],
                dst_ref=xr_c.at[pl.ds(pl.multiple_of(h * half_c + me * bc, 16), bc)],
                send_sem=sc.at[h], recv_sem=rc.at[h], device_id=where, device_id_type=MESH,
            ).start()
            if h == 0:
                pltpu.make_async_remote_copy(
                    src_ref=xs_s.at[pl.ds(dst * bs, bs)],
                    dst_ref=xr_s.at[pl.ds(me * bs, bs)],
                    send_sem=ss.at[0], recv_sem=rs.at[0], device_id=where, device_id_type=MESH,
                ).start()
            return carry

        lax.fori_loop(1, n, one, 0)
        at_m = pl.ds(pl.multiple_of(h * half_m + me * bm, 8), bm)
        at_c = pl.ds(pl.multiple_of(h * half_c + me * bc, 16), bc)
        pltpu.make_async_copy(xs_m.at[at_m], xr_m.at[at_m], rm.at[h]).start()
        pltpu.make_async_copy(xs_c.at[at_c], xr_c.at[at_c], rc.at[h]).start()
        if h == 0:
            at_s = pl.ds(me * bs, bs)
            pltpu.make_async_copy(xs_s.at[at_s], xr_s.at[at_s], rs.at[0]).start()

    for h in range(PARTS):
        send_grads(h)
    send_blocks(0)
    for r in range(1, RELAYS):
        stage(r)
        send_blocks(r)

    for h in range(PARTS):
        hand_on(h)

    inv_one = 1.0 / (1.0 - 0.9**STEP)
    inv_two = 1.0 / (1.0 - 0.95**STEP)

    def adam(h, s1, s2, tops):
        if h * RELAYS % PARTS == 0:
            r = h * RELAYS // PARTS
            drain(xr_m.at[pl.ds(r * half_m, half_m)], rm.at[r])
            drain(xr_c.at[pl.ds(r * half_c, half_c)], rc.at[r])
            xs_f[pl.ds(r * half_c, half_c), :] = xr_c[pl.ds(r * half_c, half_c), :].astype(jnp.float32)
        out, got, size, mine = second(h)
        k = h // 2
        drain(got.at[k, pl.ds(0, size - 1)], rh.at[h])
        top1, top2 = tops
        for i in range(h * cq, (h + 1) * cq):
            at = slice(i * LANES, (i + 1) * LANES)
            r, j = i // cp, i % cp
            near = slice((i - h * cq) * LANES, (i - h * cq + 1) * LANES)
            grad = out[k, mine, :, near]
            for away in range(1, size):
                grad = grad + got[k, lax.rem(mine + away, size), :, near]
            first = xs_f[pl.ds(r * half_c + j, slots, stride=2 * cp), :] * s1
            other = xs_f[pl.ds(r * half_c + cp + j, slots, stride=2 * cp), :] * s2
            old = xr_m[pl.ds(r * half_m + j, slots, stride=cp), :]
            one = 0.9 * first + 0.1 * grad
            two = 0.95 * other + 0.05 * grad * grad
            update = (one * inv_one) / (jnp.sqrt(two * inv_two) + 1e-08) + 0.1 * old
            new = old - 0.01 * update
            nm_out[0, :, at] = new
            wg[0, my_dp, :, at] = new.astype(jnp.bfloat16)
            m1_v[:, at] = one
            m2_v[:, at] = two
            top1 = jnp.maximum(top1, jnp.abs(one))
            top2 = jnp.maximum(top2, jnp.abs(two))
        return top1, top2

    def gathered(chip, c, h):
        return wg.at[0, chip * 2 + c, :, cols(h)]

    def to_chip(h, chip, y, x):
        slab = gathered(chip, my_c, h)
        return pltpu.make_async_remote_copy(
            src_ref=slab, dst_ref=slab, send_sem=sa.at[h], recv_sem=ra.at[h, chip],
            device_id=(dp_of(y, x, my_c), my_t), device_id_type=MESH,
        )

    def to_partner(h, chip):
        slab = gathered(chip, my_c, h)
        return pltpu.make_async_remote_copy(
            src_ref=slab, dst_ref=slab, send_sem=sf.at[h], recv_sem=rf.at[h],
            device_id=(partner, my_t), device_id_type=MESH,
        )

    def arrived(h, chip):
        slab = gathered(chip, my_c, h)
        pltpu.make_async_copy(slab, slab, ra.at[h, chip]).wait()
        to_partner(h, chip).start()

    across = 1 - my_x
    rows_away = [lax.rem(my_y + away, ny) for away in range(1, ny)]

    def spread(h):
        to_chip(h, my_chip, my_y, across).start()
        for y in rows_away:
            to_chip(h, my_chip, y, my_x).start()
            to_chip(h, my_chip, y, across).start()
        to_partner(h, my_chip).start()

    def relay(h):
        arrived(h, my_y * 2 + across)
        for y in rows_away:
            arrived(h, y * 2 + my_x)

    def finish(h):
        for y in rows_away:
            arrived(h, y * 2 + across)

    drain(xr_s, rs.at[0])
    scales = xr_s[:, 0, :]
    s1 = scales[:, 0:1]
    s2 = scales[:, LANES // 2:LANES // 2 + 1]
    zero = jnp.zeros((slots, LANES), jnp.float32)
    tops = (zero, zero)
    for h in range(PARTS):
        tops = adam(h, s1, s2, tops)
        spread(h)
    for h in range(PARTS - 1):
        relay(h)

    top1 = jnp.max(tops[0], axis=1, keepdims=True) + 1e-06
    top2 = jnp.max(tops[1], axis=1, keepdims=True) + 1e-06
    ns1_out[...] = jnp.sum(jnp.where(eye, top1, 0.0), axis=0, keepdims=True)
    ns2_out[...] = jnp.sum(jnp.where(eye, top2, 0.0), axis=0, keepdims=True)
    inv1 = 1.0 / top1
    inv2 = 1.0 / top2
    for j in range(chunks):
        at = slice(j * LANES, (j + 1) * LANES)
        nc1_out[0, :, at] = (m1_v[:, at] * inv1).astype(jnp.bfloat16)
        nc2_out[0, :, at] = (m2_v[:, at] * inv2).astype(jnp.bfloat16)

    relay(PARTS - 1)
    for h in range(PARTS):
        finish(h)
    for h in range(PARTS):
        out, got, size, mine = second(h)
        k = h // 2
        theirs = wg.at[0, pl.ds(0, chips), :, cols(h)]
        drain(theirs, rf.at[h])
        drain(theirs, sf.at[h])
        drain(wg.at[0, pl.ds(0, chips - 1), :, cols(h)], sa.at[h])
        drain(got.at[k, pl.ds(0, size - 1)], sh.at[h])
        group = 2 if h % 2 == 0 else ny
        drain(wg.at[0, pl.ds(0, (2 * group - 1) * (nd // (2 * group))), :, cols(h)], sg.at[h])
    for r in range(RELAYS):
        drain(xs_m.at[pl.ds(0, half_m - bm)], sm.at[r])
        drain(xs_c.at[pl.ds(0, half_c - bc)], sc.at[r])
    drain(xs_s.at[pl.ds(0, slots - bs)], ss.at[0])


def _write_out(*refs):
    sem = refs[-1]
    count = (len(refs) - 1) // 2
    copies = [pltpu.make_async_copy(refs[i], refs[count + i], sem.at[i]) for i in range(count)]
    for item in copies:
        item.start()
    for item in copies:
        item.wait()


def on_device(send_order, master, first_code, first_scale, second_code, second_scale, grads):
    arrays = (send_order, master, first_code, first_scale, second_code, second_scale, grads)
    nd = lax.axis_size("dp")
    nt = lax.axis_size("tensor")
    slots = master.shape[1]
    width = master.shape[2]
    f32, b16 = jnp.float32, jnp.bfloat16
    rows = slots * width // LANES
    dma = pltpu.SemaphoreType.DMA
    ny = nd // 4
    pairs = PARTS // 2
    wp = width // PARTS
    arrays = arrays[:6] + (grads.reshape(ny, 2, 2, slots, width),)
    grant = slots * width * (40 + 6 * nd) + slots * 4096 + 6 * 1024 * 1024
    results = (
        ((1, slots, width), f32),
        ((1, slots, width), b16),
        ((1, slots), f32),
        ((1, slots, width), b16),
        ((1, slots), f32),
        ((1, nd, slots, width), b16),
    )
    held = pl.pallas_call(
        functools.partial(_kernel, nd, nt, slots, width),
        out_shape=tuple(pltpu.VMEM(*item) for item in results),
        in_specs=[pl.BlockSpec(memory_space=pltpu.HBM)] * 7,
        out_specs=[pl.BlockSpec(memory_space=pltpu.VMEM)] * 6,
        scratch_shapes=[
            pltpu.VMEM((1, slots), jnp.int32),
            pltpu.VMEM((1, slots), f32),
            pltpu.VMEM((1, slots), f32),
            pltpu.VMEM((slots, width), f32),
            pltpu.VMEM((slots, width), b16),
            pltpu.VMEM((slots, width), b16),
            pltpu.VMEM((rows, LANES), f32),
            pltpu.VMEM((2 * rows, LANES), f32),
            pltpu.VMEM((2 * rows, LANES), b16),
            pltpu.VMEM((slots, 1, LANES), f32),
            pltpu.VMEM((rows, LANES), f32),
            pltpu.VMEM((2 * rows, LANES), b16),
            pltpu.VMEM((slots, 1, LANES), f32),
            pltpu.VMEM((pairs, 2, 2, ny, slots, wp), b16),
            pltpu.VMEM((pairs, ny, 2, 2, slots, wp), b16),
            pltpu.VMEM((pairs, ny, slots, wp), f32),
            pltpu.VMEM((pairs, 2, slots, wp), f32),
            pltpu.VMEM((pairs, ny, slots, wp), f32),
            pltpu.VMEM((pairs, 2, slots, wp), f32),
            pltpu.VMEM((slots, width), f32),
            pltpu.VMEM((slots, width), f32),
            dma((6,)),
            dma((RELAYS,)), dma((RELAYS,)), dma((1,)), dma((PARTS,)),
            dma((RELAYS,)), dma((RELAYS,)), dma((1,)), dma((PARTS,)),
            dma((PARTS,)), dma((PARTS,)),
            dma((PARTS, 2 * ny)), dma((PARTS,)), dma((PARTS,)), dma((PARTS,)),
        ],
        compiler_params=pltpu.CompilerParams(collective_id=0, has_side_effects=True, vmem_limit_bytes=grant),
        name="relayout_adam",
    )(*(pltpu.with_memory_space_constraint(item, pltpu.HBM) for item in arrays))
    return pl.pallas_call(
        _write_out,
        out_shape=tuple(jax.ShapeDtypeStruct(*item) for item in results),
        in_specs=[pl.BlockSpec(memory_space=pltpu.VMEM)] * len(results),
        out_specs=[pl.BlockSpec(memory_space=pltpu.HBM)] * len(results),
        scratch_shapes=[dma((len(results),))],
        compiler_params=pltpu.CompilerParams(vmem_limit_bytes=2 * 1024 * 1024),
        name="write_out",
    )(*(pltpu.with_memory_space_constraint(item, pltpu.VMEM) for item in held))


def solution(mesh):
    placed = (
        P(("dp", "tensor"), None),
        P(("dp", "tensor"), None, None),
        P(("dp", "tensor"), None, None),
        P(("dp", "tensor"), None),
        P(("dp", "tensor"), None, None),
        P(("dp", "tensor"), None),
        P("dp", "tensor", None, None, None),
    )
    return jax.shard_map(
        on_device,
        mesh=mesh,
        in_specs=placed,
        out_specs=(
            P(("dp", "tensor"), None, None),
            P(("dp", "tensor"), None, None),
            P(("dp", "tensor"), None),
            P(("dp", "tensor"), None, None),
            P(("dp", "tensor"), None),
            P("tensor", None, None, None),
        ),
        check_vma=False,
    )
```
